32 devices in a mesh: grp: 2 (over y), dp: 16 (over z, x, core).
Axes of the slice: x: 2, y: 2, z: 4, core: 2. Of those that a mesh axis runs over, the one named last changes fastest.
Arguments:
- teacher_states: bfloat16 [2, 4096, 6144], P(None, 'dp', 'grp'), may hold values from -18.5 to 18.5
- student_features: bfloat16 [2, 4096, 1024], P(None, 'dp'), may hold values from -13 to 13
- w_first: bfloat16 [1024, 1024], replicated, may hold values from -0.1875 to 0.1875
- w_second: bfloat16 [1024, 1024], replicated, may hold values from -0.1875 to 0.1875
Outputs:
- correlation: float32 [1024, 6144], P('dp', 'grp')
The draws below stay inside these ranges and needn't reach their ends.
All inputs are finite; a program needn't handle non-finite values.
Results may differ from the reference program's by a relative error of at most 0.0003.
Values may be sent and summed in bfloat16 or wider, within the bound.
No kernel may reach another device: no remote copies, remote signals or barrier semaphores. Data moves between devices by JAX's collectives and lax.ppermute only.
A program may use at most 128 MiB of HBM per device.

```python
import math
import jax
import jax.numpy as jnp
from jax import lax

DT = 6144
DS = 1024
MB = 2
TOKENS = 4096


def draw_teacher_states(key, part):
    keys = jax.random.split(jax.random.fold_in(key, 11), 4)
    offsets = jax.random.uniform(keys[0], (DT,), jnp.float32, -1.0, 1.0)
    slopes = jax.random.uniform(keys[1], (DT,), jnp.float32, -1.5, 1.5)
    scales = jnp.exp(jax.random.uniform(keys[2], (DT,), jnp.float32, math.log(0.3), math.log(3.0)))
    ramp = 3.0 * jnp.arange(TOKENS, dtype=jnp.float32) / TOKENS - 1.5
    noise = jnp.clip(jax.random.normal(keys[3], (MB, TOKENS, DT), jnp.float32), -5.0, 5.0)
    values = offsets + slopes * ramp[:, None] + scales * noise
    return values.astype(jnp.bfloat16)


def draw_student_features(key, part):
    keys = jax.random.split(jax.random.fold_in(key, 12), 4)
    offsets = jax.random.uniform(keys[0], (DS,), jnp.float32, -1.0, 1.0)
    slopes = jax.random.uniform(keys[1], (DS,), jnp.float32, -1.0, 1.0)
    scales = jnp.exp(jax.random.uniform(keys[2], (DS,), jnp.float32, math.log(0.5), math.log(2.0)))
    ramp = 3.0 * jnp.arange(TOKENS, dtype=jnp.float32) / TOKENS - 1.5
    noise = jnp.clip(jax.random.normal(keys[3], (MB, TOKENS, DS), jnp.float32), -5.0, 5.0)
    values = offsets + slopes * ramp[:, None] + scales * noise
    return values.astype(jnp.bfloat16)


def normal_values(own_key, dims, deviation, limit, kind=jnp.bfloat16):
    return jnp.clip(deviation * jax.random.normal(own_key, dims, jnp.float32), -limit, limit).astype(kind)


def setup_inputs(seed: int = 0) -> dict:
    key_list = jax.random.split(jax.random.key(seed), 5)
    return {
        "teacher_states": draw_teacher_states(jax.random.fold_in(key_list[4], 71), 0),
        "student_features": draw_student_features(jax.random.fold_in(key_list[4], 71), 0),
        "w_first": normal_values(key_list[2], (DS, DS), DS ** -0.5, 0.1875),
        "w_second": normal_values(key_list[3], (DS, DS), DS ** -0.5, 0.1875),
    }


EPSILON = 1e-06

def normalize_rows(states):
    values = states.astype(jnp.float32)
    row_mean = lax.optimization_barrier(jnp.sum(values, axis=1)) / DT
    row_var = lax.optimization_barrier(jnp.sum(values * values, axis=1)) / DT - row_mean * row_mean
    return (values - row_mean[:, None]) * lax.rsqrt(row_var + EPSILON)[:, None]

def student_side(features, w_first, w_second):
    hidden = jax.nn.gelu(jnp.dot(features, w_first, preferred_element_type=jnp.float32)).astype(jnp.bfloat16)
    projected = jnp.dot(hidden, w_second, preferred_element_type=jnp.float32)
    number = features.shape[0]
    col_mean = lax.optimization_barrier(jnp.sum(projected, axis=0)) / number
    col_var = lax.optimization_barrier(jnp.sum(projected * projected, axis=0)) / number - col_mean * col_mean
    return ((projected - col_mean) * lax.rsqrt(col_var + EPSILON)).astype(jnp.bfloat16)

def one_batch(states, features, w_first, w_second):
    student_z = student_side(features, w_first, w_second)
    block = math.gcd(TOKENS, 2048)
    blocks = TOKENS // block
    state_blocks = states.reshape(blocks, block, DT)
    student_blocks = student_z.reshape(blocks, block, DS)

    def add_power(carry, slab):
        normed = normalize_rows(slab)
        return (carry + lax.optimization_barrier(jnp.sum(normed * normed, axis=0)), None)
    power, _ = lax.scan(add_power, jnp.zeros((DT,), jnp.float32), state_blocks)
    scale = lax.rsqrt(power / TOKENS + EPSILON)

    def add_product(carry, pair):
        slab, student_slab = pair
        teacher_z = (normalize_rows(slab) * scale).astype(jnp.bfloat16)
        product = jnp.dot(student_slab.astype(jnp.float32).T, teacher_z.astype(jnp.float32), precision=lax.Precision.HIGHEST, preferred_element_type=jnp.float32)
        return (carry + product, None)
    result, _ = lax.scan(add_product, jnp.zeros((DS, DT), jnp.float32), (state_blocks, student_blocks))
    return result

def reference(teacher_states, student_features, w_first, w_second):
    running = jnp.zeros((DS, DT), jnp.float32)
    for batch_index in range(MB):
        running = running + one_batch(teacher_states[batch_index], student_features[batch_index], w_first, w_second)
    return running * (1.0 / math.sqrt(MB * TOKENS))
```

```python
import math

import jax
import jax.numpy as jnp
from jax import lax
from jax.sharding import PartitionSpec as P

EPSILON = 1e-06
LIFT = 256.0
CHUNKS = ((0.25, False), (0.25, True), (0.25, False), (0.25, False))


def swap(value, axis, bit):
    size = lax.axis_size(axis)
    return lax.ppermute(value, axis, [(d, d ^ bit) for d in range(size)])


def shards(teacher, features, w_first, w_second):
    mb, tok, width = teacher.shape
    ds = w_second.shape[1]
    n = lax.axis_size("dp")
    grp = lax.axis_size("grp")
    me = lax.axis_index("dp")
    levels = n.bit_length() - 1
    hops = levels - 1
    rows = ds // n
    token_total = tok * n
    blocks = n // 2

    partner_x = swap(teacher, "dp", 1)

    x = teacher.astype(jnp.float32)
    sums = jnp.stack([jnp.sum(x, axis=2), jnp.sum(x * x, axis=2)])
    sums = sums + swap(sums, "grp", 1)
    mean = sums[0] / (width * grp)
    rstd = lax.rsqrt(sums[1] / (width * grp) - mean * mean + EPSILON)

    hidden = jax.nn.gelu(
        jnp.dot(features.reshape(mb * tok, -1), w_first, preferred_element_type=jnp.float32)
    ).astype(jnp.bfloat16)
    partner_hidden = swap(hidden, "dp", 1)

    index = jnp.arange(blocks)
    distance = jnp.zeros_like(index)
    for h in range(hops):
        distance = distance + (((index >> (hops - 1 - h)) & 1) << (h + 1))
    owner = me ^ distance
    source = (owner[:, None] * rows + jnp.arange(rows)[None, :]).reshape(-1)
    select = (source[:, None] == jnp.arange(ds)[None, :]).astype(jnp.bfloat16)
    w_sel = lax.dot_general(
        select, w_second, (((1,), (1,)), ((), ())), preferred_element_type=jnp.float32
    ).astype(jnp.bfloat16)
    project = lambda h: lax.dot_general(
        w_sel, h, (((1,), (1,)), ((), ())), preferred_element_type=jnp.float32
    ).reshape(blocks * rows, mb, tok)
    proj = project(hidden), project(partner_hidden)
    s1 = sum(jnp.sum(p, axis=2) for p in proj)
    s2 = sum(jnp.sum(p * p, axis=2) for p in proj)
    student = jnp.stack([s1, s2])

    normed = (x - mean[..., None]) * rstd[..., None]
    power = jnp.sum(normed * normed, axis=1)
    first = jnp.concatenate([power.reshape(-1), mean.reshape(-1), rstd.reshape(-1)])
    got = swap(first, "dp", 1)
    count = mb * width
    power = power.reshape(-1) + got[:count]
    p_mean = got[count : count + mb * tok].reshape(mb, tok)
    p_rstd = got[count + mb * tok :].reshape(mb, tok)

    bits = (2,) * hops
    for h in range(hops):
        got = swap(jnp.concatenate([power, student.reshape(-1)]), "dp", 2 << h)
        power = power + got[:count]
        theirs = got[count:].reshape((2,) + bits + (rows, mb))
        student = (student.reshape((2,) + bits + (rows, mb)) + jnp.flip(theirs, axis=1 + h))
    student = student.reshape(2, blocks * rows, mb)
    col_mean = student[0] / token_total
    col_scale = lax.rsqrt(student[1] / token_total - col_mean * col_mean + EPSILON)
    z = [
        ((p - col_mean[..., None]) * col_scale[..., None])
        .astype(jnp.bfloat16)
        .reshape(blocks * rows, mb * tok)
        for p in proj
    ]
    scale = lax.rsqrt(power.reshape(mb, 1, width) / token_total + EPSILON)
    factor = LIFT / math.sqrt(mb * token_total)

    pieces = []
    start = 0
    for share, late in CHUNKS:
        size = int(width * share)
        cols = slice(start, start + size)
        start += size
        product = None
        for zi, xi, mi, ri in (
            (z[0], teacher, mean, rstd),
            (z[1], partner_x, p_mean, p_rstd),
        ):
            tz = (
                (xi[:, :, cols].astype(jnp.float32) - mi[..., None]) * ri[..., None] * scale[:, :, cols]
            ).astype(jnp.bfloat16)
            part = jnp.dot(zi, tz.reshape(mb * tok, size), preferred_element_type=jnp.float32)
            product = part if product is None else product + part
        product = (product * factor).reshape(bits + (rows, size))
        order = list(range(1, hops)) + [0] if late else list(range(hops))
        held = product
        for h in order:
            keep = lax.index_in_dim(held, 0, h, keepdims=True)
            send = lax.index_in_dim(held, 1, h, keepdims=True).astype(jnp.float16)
            held = keep + swap(send, "dp", 2 << h).astype(jnp.float32)
        pieces.append(held.reshape(rows, size) * (1.0 / LIFT))
    return jnp.concatenate(pieces, axis=1)


def solution(mesh):
    placed = (P(None, "dp", "grp"), P(None, "dp", None), P(), P())
    return jax.shard_map(
        shards, mesh=mesh, in_specs=placed, out_specs=P("dp", "grp"), check_vma=False
    )
```

```python
import functools
import math

import jax
import jax.numpy as jnp
from jax import lax
from jax.experimental import pallas as pl
from jax.experimental.pallas import tpu as pltpu
from jax.sharding import PartitionSpec as P

EPSILON = 1e-06
LIFT = 256.0
LANES = 128
ROWS = 8
CHUNKS = ((1024, False), (512, True), (1024, False), (512, False))
IN_VMEM = pl.BlockSpec(memory_space=pltpu.VMEM)


def call(body, out_shapes, args, flops=0, moved=0, **kw):
    return pl.pallas_call(
        body,
        out_shape=[jax.ShapeDtypeStruct(s, t) for s, t in out_shapes],
        cost_estimate=pl.CostEstimate(flops=flops, bytes_accessed=moved, transcendentals=0),
        compiler_params=pltpu.CompilerParams(vmem_limit_bytes=48 << 20),
        **kw,
    )(*args)


def swap(value, axis, bit):
    size = lax.axis_size(axis)
    return lax.ppermute(value, axis, [(d, d ^ bit) for d in range(size)])


def fold_lanes(tile):
    total = tile[:, :LANES]
    for start in range(LANES, tile.shape[1], LANES):
        total = total + tile[:, start : start + LANES]
    return total


def as_row(partial):
    return jnp.sum(partial.T, axis=0, keepdims=True)


def as_column(row):
    return jnp.broadcast_to(row, (LANES, LANES)).T


def token_sums_body(x_ref, out_ref):
    values = x_ref[0].astype(jnp.float32)
    first = as_row(fold_lanes(values))
    second = as_row(fold_lanes(values * values))
    out_ref[...] = jnp.concatenate(
        [first, second, jnp.zeros((ROWS - 2, first.shape[1]), jnp.float32)], axis=0
    )


def token_sums(x):
    mb, tok, width = x.shape
    per = tok // LANES
    return pl.pallas_call(
        token_sums_body,
        grid=(mb * per,),
        in_specs=[pl.BlockSpec((1, LANES, width), lambda i: (i // per, i % per, 0))],
        out_specs=pl.BlockSpec((ROWS, LANES), lambda i: (0, i)),
        out_shape=jax.ShapeDtypeStruct((ROWS, mb * tok), jnp.float32),
        cost_estimate=pl.CostEstimate(flops=4 * x.size, bytes_accessed=2 * x.size, transcendentals=0),
    )(x)


def moments(sums, count):
    mean = sums[0:1] / count
    return mean, lax.rsqrt(sums[1:2] / count - mean * mean + EPSILON)


def power_body(count, x_ref, mine_ref, theirs_ref, out_ref, acc_ref):
    mb = pl.program_id(0)
    block = pl.program_id(1)
    per = pl.num_programs(1)
    width = x_ref.shape[2]
    sums = mine_ref[0:2, :] + theirs_ref[0:2, :]
    mean, rstd = moments(sums, count)
    mean, rstd = as_column(mean), as_column(rstd)

    @pl.when(block == 0)
    def _():
        acc_ref[...] = jnp.zeros_like(acc_ref)

    for start in range(0, width, LANES):
        values = x_ref[0, :, start : start + LANES].astype(jnp.float32)
        normed = (values - mean) * rstd
        square = (normed * normed).reshape(LANES // ROWS, ROWS, LANES)
        acc_ref[:, start : start + LANES] += jnp.sum(square, axis=0)

    quarter = ROWS // 2
    size = width // quarter

    @pl.when(block == per - 1)
    def _():
        line = jnp.sum(acc_ref[...], axis=0, keepdims=True)
        for m in range(2):

            @pl.when(mb == m)
            def _():
                for q in range(quarter):
                    out_ref[m * quarter + q : m * quarter + q + 1, :size] = line[:, q * size : (q + 1) * size]

    for stat in range(2):
        for m in range(2):
            for b in range(ROWS // 4):

                @pl.when((mb == m) & (block == b))
                def _():
                    r = stat * (ROWS // 2) + m * (ROWS // 4) + b
                    out_ref[r : r + 1, size:] = sums[stat : stat + 1, :]


def power_sums(x, mine, theirs, count):
    mb, tok, width = x.shape
    per = tok // LANES
    assert mb == 2 and per * 2 == ROWS // 2
    token = pl.BlockSpec((ROWS, LANES), lambda m, i: (0, m * per + i))
    shape = (ROWS, width // (ROWS // 2) + LANES)
    return pl.pallas_call(
        functools.partial(power_body, count),
        grid=(mb, per),
        in_specs=[pl.BlockSpec((1, LANES, width), lambda m, i: (m, i, 0)), token, token],
        out_specs=pl.BlockSpec(shape, lambda m, i: (0, 0)),
        out_shape=jax.ShapeDtypeStruct(shape, jnp.float32),
        scratch_shapes=[pltpu.VMEM((ROWS, width), jnp.float32)],
        cost_estimate=pl.CostEstimate(flops=5 * x.size, bytes_accessed=2 * x.size, transcendentals=0),
    )(x, mine, theirs)


def project_body(mb, sel_ref, own_ref, partner_ref, proj_ref, sums_ref):
    feats = sel_ref.shape[0]
    tok = own_ref.shape[0] // mb
    for side, ref in enumerate((own_ref, partner_ref)):
        proj_ref[:, side * mb * tok : (side + 1) * mb * tok] = lax.dot_general(
            sel_ref[...], ref[...], (((1,), (1,)), ((), ())), preferred_element_type=jnp.float32
        )
    half = feats // 2
    for m in range(mb):
        pieces = [proj_ref[:, (side * mb + m) * tok : (side * mb + m + 1) * tok] for side in range(2)]
        one = as_row(fold_lanes(pieces[0]) + fold_lanes(pieces[1]))
        two = as_row(fold_lanes(pieces[0] * pieces[0]) + fold_lanes(pieces[1] * pieces[1]))
        for stat, line in enumerate((one, two)):
            r = (stat * mb + m) * 2
            sums_ref[r : r + 1, :] = line[:, :half]
            sums_ref[r + 1 : r + 2, :] = line[:, half:]


def join_body(power_ref, got_ref, sums_ref, out_ref):
    size = power_ref.shape[1] - LANES
    out_ref[:, :size] = power_ref[:, :size] + got_ref[:, :size]
    out_ref[:, size:] = sums_ref[...]


def hop_body(stride, half, mine_ref, got_ref, out_ref):
    size = out_ref.shape[1] - half
    out_ref[:, :size] = mine_ref[:, :size] + got_ref[:, :size]
    theirs = got_ref[:, size:]
    if stride >= half:
        row = lax.broadcasted_iota(jnp.int32, theirs.shape, 0)
        theirs = jnp.where(row % 2 == 1, pltpu.roll(theirs, 1, 0), pltpu.roll(theirs, ROWS - 1, 0))
    else:
        lane = lax.broadcasted_iota(jnp.int32, theirs.shape, 1)
        theirs = jnp.where(
            (lane & stride) != 0, pltpu.roll(theirs, stride, 1), pltpu.roll(theirs, half - stride, 1)
        )
    out_ref[:, size:] = mine_ref[:, size:] + theirs


def student_body(mb, total, proj_ref, hop_ref, own_ref, partner_ref, scale_ref):
    feats = proj_ref.shape[0]
    half = feats // 2
    size = hop_ref.shape[1] - half
    tok = own_ref.shape[1] // mb
    quarter = ROWS // mb
    for m in range(mb):
        for q in range(quarter):
            scale_ref[m : m + 1, q * size : (q + 1) * size] = lax.rsqrt(
                hop_ref[m * quarter + q : m * quarter + q + 1, :size] / total + EPSILON
            )
        for block in range(feats // LANES):
            rows = slice(block * LANES, (block + 1) * LANES)
            part, lane = divmod(block * LANES, half)
            lines = []
            for stat in range(2):
                r = (stat * mb + m) * 2 + part
                lines.append(hop_ref[r : r + 1, size + lane : size + lane + LANES] / total)
            spread = lax.rsqrt(lines[1] - lines[0] * lines[0] + EPSILON)
            mean, spread = as_column(lines[0]), as_column(spread)
            for side, ref in enumerate((own_ref, partner_ref)):
                for start in range(0, tok, LANES):
                    at = (side * mb + m) * tok + start
                    ref[rows, m * tok + start : m * tok + start + LANES] = (
                        (proj_ref[rows, at : at + LANES] - mean) * spread
                    ).astype(jnp.bfloat16)


def columns_body(count, mine_ref, theirs_ref, packed_ref, mean_ref, rstd_ref):
    tokens = mine_ref.shape[1]
    size = packed_ref.shape[1] - LANES
    for block in range(tokens // LANES):
        sums = (
            mine_ref[0:2, block * LANES : (block + 1) * LANES]
            + theirs_ref[0:2, block * LANES : (block + 1) * LANES]
        )
        other = jnp.concatenate(
            [packed_ref[block : block + 1, size:], packed_ref[block + ROWS // 2 : block + ROWS // 2 + 1, size:]],
            axis=0,
        )
        for side, pair in enumerate((sums, other)):
            mean, rstd = moments(pair, count)
            at = side * tokens + block * LANES
            mean_ref[at : at + LANES, :] = as_column(mean)
            rstd_ref[at : at + LANES, :] = as_column(rstd)


def product_body(
    mb, start, width, factor, own_z, partner_z, own_x, partner_x, mean_ref, rstd_ref, scale_ref, keep_ref, send_ref, tz_ref
):
    tokens = own_z.shape[1]
    tok = tokens // mb
    total = None
    for side, (z_ref, x_ref) in enumerate(((own_z, own_x), (partner_z, partner_x))):
        for m in range(mb):
            for block in range(tok // LANES):
                at = m * tok + block * LANES
                mean = mean_ref[side * tokens + at : side * tokens + at + LANES, :]
                rstd = rstd_ref[side * tokens + at : side * tokens + at + LANES, :]
                for c in range(0, width, LANES):
                    values = x_ref[
                        m, block * LANES : (block + 1) * LANES, start + c : start + c + LANES
                    ].astype(jnp.float32)
                    tz_ref[side, at : at + LANES, c : c + LANES] = (
                        (values - mean) * rstd * scale_ref[m : m + 1, start + c : start + c + LANES]
                    ).astype(jnp.bfloat16)
    half = own_z.shape[0] // 2
    for part, ref in ((1, send_ref), (0, keep_ref)):
        rows = slice(part * half, (part + 1) * half)
        total = jnp.dot(own_z[rows, :], tz_ref[0], preferred_element_type=jnp.float32)
        total = total + jnp.dot(partner_z[rows, :], tz_ref[1], preferred_element_type=jnp.float32)
        ref[...] = total * factor


def shards(teacher, features, w_first, w_second):
    mb, tok, width = teacher.shape
    ds = w_second.shape[1]
    n = lax.axis_size("dp")
    grp = lax.axis_size("grp")
    me = lax.axis_index("dp")
    hops = n.bit_length() - 2
    rows = ds // n
    token_total = tok * n
    blocks = n // 2
    feats = blocks * rows
    half = feats // 2
    tokens = mb * tok
    count = width * grp

    partner_x = swap(teacher, "dp", 1)
    mine = token_sums(teacher)
    theirs = swap(mine, "grp", 1)

    hidden = jax.nn.gelu(
        jnp.dot(features.reshape(tokens, -1), w_first, preferred_element_type=jnp.float32)
    ).astype(jnp.bfloat16)
    partner_hidden = swap(hidden, "dp", 1)

    index = jnp.arange(blocks)
    distance = jnp.zeros_like(index)
    for h in range(hops):
        distance = distance + (((index >> (hops - 1 - h)) & 1) << (h + 1))
    owner = me ^ distance
    source = (owner[:, None] * rows + jnp.arange(rows)[None, :]).reshape(-1)
    select = (source[:, None] == jnp.arange(ds)[None, :]).astype(jnp.bfloat16)
    w_sel = lax.dot_general(
        select, w_second, (((1,), (1,)), ((), ())), preferred_element_type=jnp.float32
    ).astype(jnp.bfloat16)

    power = power_sums(teacher, mine, theirs, count)
    got = swap(power, "dp", 1)
    proj, student = call(
        functools.partial(project_body, mb),
        [((feats, 2 * tokens), jnp.float32), ((ROWS, half), jnp.float32)],
        (w_sel, hidden, partner_hidden),
        flops=4 * feats * tokens * ds,
        moved=8 * feats * tokens,
    )
    (total,) = call(join_body, [((ROWS, power.shape[1] - LANES + half), jnp.float32)], (power, got, student))
    mean_b, rstd_b = call(
        functools.partial(columns_body, count),
        [((2 * tokens, LANES), jnp.float32)] * 2,
        (mine, theirs, got),
        moved=8 * tokens * LANES,
    )
    for h in range(hops):
        (total,) = call(
            functools.partial(hop_body, feats >> (h + 1), half),
            [(total.shape, jnp.float32)],
            (total, swap(total, "dp", 2 << h)),
        )
    own_z, partner_z, scale = call(
        functools.partial(student_body, mb, token_total),
        [((feats, tokens), jnp.bfloat16)] * 2 + [((mb, width), jnp.float32)],
        (proj, total),
        moved=8 * feats * tokens,
    )
    factor = LIFT / math.sqrt(mb * token_total)

    bits = (2,) * (hops - 1)
    pieces = []
    start = 0
    for size, late in CHUNKS:
        keep, send = pl.pallas_call(
            functools.partial(product_body, mb, start, size, factor),
            out_shape=[jax.ShapeDtypeStruct((half, size), jnp.float32)] * 2,
            scratch_shapes=[pltpu.VMEM((2, tokens, size), jnp.bfloat16)],
            cost_estimate=pl.CostEstimate(
                flops=4 * feats * tokens * size, bytes_accessed=4 * feats * size, transcendentals=0
            ),
            compiler_params=pltpu.CompilerParams(vmem_limit_bytes=48 << 20),
        )(own_z, partner_z, teacher, partner_x, mean_b, rstd_b, scale)
        start += size
        keep = keep.reshape((1,) + bits + (rows, size))
        send = send.reshape((1,) + bits + (rows, size))
        if late:
            held = jnp.concatenate([keep, send], axis=0)
        else:
            held = keep + swap(send.astype(jnp.float16), "dp", 2).astype(jnp.float32)
        order = list(range(1, hops)) + ([0] if late else [])
        for h in order:
            kept = lax.index_in_dim(held, 0, h, keepdims=True)
            sent = lax.index_in_dim(held, 1, h, keepdims=True).astype(jnp.float16)
            held = kept + swap(sent, "dp", 2 << h).astype(jnp.float32)
        pieces.append(held.reshape(rows, size) * (1.0 / LIFT))
    return jnp.concatenate(pieces, axis=1)


def solution(mesh):
    placed = (P(None, "dp", "grp"), P(None, "dp", None), P(), P())
    return jax.shard_map(
        shards, mesh=mesh, in_specs=placed, out_specs=P("dp", "grp"), check_vma=False
    )
```
